256 devices in a mesh: dom: 64 (over x, z_lo, y, core), band: 4 (over z_hi).
Axes of the slice: x: 4, y: 4, z: 8 (z_hi: 4, z_lo: 2; z = z_hi * 2 + z_lo), core: 2. Of those that a mesh axis runs over, the one named last changes fastest.
Arguments:
- states: float32 [12288, 1536], P('dom', 'band'), may hold values from -6 to 6
- inv_mass: float32 [12288], P('dom'), may hold values from 0.5 to 2
- cell_ham: float32 [320, 343, 343], P('dom'), as said below
- cell_nodes: int32 [320, 343], P('dom'), may hold values from 0 to 287, as said below
- send_up: int32 [3072], P('dom'), may hold values from 0 to 191, as said below
- send_down: int32 [3072], P('dom'), may hold values from 0 to 191, as said below
- owner: int32 [64], replicated, may hold values from 0 to 63, each once
- rotation_store: float32 [1536, 1536], P('dom'), may hold values from -0.15625 to 0.15625
Outputs:
- rotated: float32 [12288, 1536], P('dom', 'band')
The draws below stay inside these ranges and needn't reach their ends.
Inputs may be any that keep to these rules, and one draw needn't show every extreme that they name: `cell_ham`: each cell's matrix is symmetric. `cell_nodes`: each domain's cells name every one of its extended nodes at least once. `send_up`: the 48 entries of one domain are distinct. `send_down`: the 48 entries of one domain are distinct. `owner`: a permutation.
All inputs are finite; a program needn't handle non-finite values.
Results may differ from the reference program's by a relative error of at most 0.00007.
Values sent between devices are 32-bit elements; how exact they have to be, the bound alone decides.
A program may use at most 64 MiB of HBM per device.

```python
import math
import jax
import jax.numpy as jnp
from jax import lax

STATES = 1536
CELL_NODES = 343
OWNED_NODES = 192
GHOST_NODES = 48
DOMAIN_CELLS = 5
DOMAINS = 64
ALL_NODES = 12288
ALL_GHOSTS = 3072
ALL_CELLS = 320
PANEL_ROWS = 24
N_DOM = 64


def swap_entries(values, left_spot, right_spot):
    left_value = values[left_spot]
    right_value = values[right_spot]
    return values.at[left_spot].set(right_value).at[right_spot].set(left_value)


def interface_lists(key, salt):
    domains = ALL_GHOSTS // GHOST_NODES
    base_key = jax.random.fold_in(key, salt)
    domain_keys = jax.random.split(base_key, domains)
    spot_key = jax.random.fold_in(base_key, 7)
    perms = jax.vmap(lambda one_key: jax.random.permutation(one_key, OWNED_NODES))(domain_keys)
    high_spot = jax.random.randint(jax.random.fold_in(spot_key, 1), (), 0, GHOST_NODES)
    step_size = jax.random.randint(jax.random.fold_in(spot_key, 2), (), 0, GHOST_NODES - 1)
    low_spot = (high_spot + 1 + step_size) % GHOST_NODES
    leading = perms[0]
    leading = swap_entries(leading, jnp.argmax(leading == OWNED_NODES - 1), high_spot)
    leading = swap_entries(leading, jnp.argmax(leading == 0), low_spot)
    perms = perms.at[0].set(leading)
    return perms[:, :GHOST_NODES].reshape(-1).astype(jnp.int32)


def draw_send_up(key, part):
    return interface_lists(key, 11)


def draw_send_down(key, part):
    return interface_lists(key, 12)


def draw_cell_nodes(key, part):
    domains = ALL_CELLS // DOMAIN_CELLS
    extended = OWNED_NODES + 2 * GHOST_NODES
    slot_count = DOMAIN_CELLS * CELL_NODES
    copies = -(-slot_count // extended)

    def one_domain(domain_key):
        pieces_list = [jax.random.permutation(jax.random.fold_in(domain_key, copy_index), extended) for copy_index in range(copies)]
        return jnp.concatenate(pieces_list)[:slot_count].reshape(DOMAIN_CELLS, CELL_NODES)
    domain_keys = jax.random.split(jax.random.fold_in(key, 21), domains)
    table = jax.vmap(one_domain)(domain_keys)
    return table.reshape(ALL_CELLS, CELL_NODES).astype(jnp.int32)


def draw_cell_ham(key, part):
    base_key = jax.random.fold_in(key, 31)
    shape = (ALL_CELLS, CELL_NODES, CELL_NODES)
    base = jax.random.normal(base_key, shape, jnp.float32)
    symmetric = (base + jnp.swapaxes(base, 1, 2)) / jnp.sqrt(2.0 * CELL_NODES)
    return jnp.clip(symmetric, -0.5, 0.5).astype(jnp.float32)


def levels(key, extent, shards, smallest, top_value):
    def one(axis_at, shards_of):
        heights = jax.random.uniform(jax.random.fold_in(jax.random.fold_in(key, 6), axis_at), (shards_of,), jnp.float32, smallest / len(shards), top_value / len(shards))
        return jnp.repeat(jnp.exp(heights), extent[axis_at] // shards_of).reshape((-1,) + (1,) * (len(extent) - axis_at - 1))

    loudness = one(*shards[0])
    for cut in shards[1:]:
        loudness = loudness * one(*cut)
    return loudness


def normal_values(rng, extent, scale, bound, cuts=(), held_as=jnp.bfloat16):
    entries = jax.random.normal(rng, extent, jnp.float32) * scale
    if len(cuts) > 0:
        entries = levels(rng, extent, cuts, -0.22, 0.18) * entries
    return jnp.clip(entries, min=-bound, max=bound).astype(held_as)


def setup_inputs(seed: int = 0) -> dict:
    arg_keys = jax.random.split(jax.random.key(seed), 9)
    states = normal_values(arg_keys[0], (ALL_NODES, STATES), 1.0, 6.0, ((0, 64), (1, 4)), jnp.float32)
    inv_mass = jnp.clip(jnp.exp(math.log(2.0) - 1.3862944 * jax.random.uniform(arg_keys[1], (ALL_NODES,), jnp.float32) ** levels(arg_keys[1], (ALL_NODES,), ((0, 64),), -0.2, 0.2)), 0.5, 2.0)
    cell_ham = draw_cell_ham(jax.random.fold_in(arg_keys[8], 71), 0)
    cell_nodes = draw_cell_nodes(jax.random.fold_in(arg_keys[8], 71), 0)
    send_up = draw_send_up(jax.random.fold_in(arg_keys[8], 71), 0)
    send_down = draw_send_down(jax.random.fold_in(arg_keys[8], 71), 0)
    owner = jax.random.permutation(arg_keys[6], DOMAINS).astype(jnp.int32)
    rotation_store = normal_values(arg_keys[7], (STATES, STATES), STATES ** -0.5, 0.15625, ((0, 64),), jnp.float32)
    return dict(states=states, inv_mass=inv_mass, cell_ham=cell_ham, cell_nodes=cell_nodes, send_up=send_up, send_down=send_down, owner=owner, rotation_store=rotation_store)


filter_center = 2.5
filter_half = 3.5
spectrum_floor = -4.0
sigma_one = filter_half / (spectrum_floor - filter_center)
sigma_two = 1.0 / (2.0 / sigma_one - sigma_one)


def apply_operator(values, inv_mass, cell_ham, cell_nodes, send_up, send_down):
    domains = N_DOM
    owned_count = OWNED_NODES
    ghost_count = GHOST_NODES
    width = values.shape[1]
    scaled = (values * inv_mass[:, None]).reshape(domains, owned_count, width)
    upper_lists = send_up.reshape(domains, ghost_count)
    lower_lists = send_down.reshape(domains, ghost_count)
    select_rows = jax.vmap(lambda values_block, index_list: values_block[index_list])
    lower_ghosts = jnp.roll(select_rows(scaled, upper_lists), 1, axis=0)
    upper_ghosts = jnp.roll(select_rows(scaled, lower_lists), -1, axis=0)
    extended = jnp.concatenate([scaled, lower_ghosts, upper_ghosts], axis=1)
    hams = cell_ham.reshape(domains, DOMAIN_CELLS, CELL_NODES, CELL_NODES)
    node_table = cell_nodes.reshape(domains, DOMAIN_CELLS, CELL_NODES)

    def one_domain(inputs):
        extended_block, ham_block, node_block = inputs
        gathered = extended_block[node_block]
        products = jnp.einsum("cij,cjs->cis", ham_block, gathered, precision=lax.Precision.HIGHEST, preferred_element_type=jnp.float32)
        empty = jnp.zeros((owned_count + 2 * ghost_count, width), jnp.float32)
        return empty.at[node_block.reshape(-1)].add(products.reshape(-1, width))

    assembled = lax.map(one_domain, (extended, hams, node_table))
    from_upper = jnp.roll(assembled[:, owned_count:owned_count + ghost_count], -1, axis=0)
    from_lower = jnp.roll(assembled[:, owned_count + ghost_count:], 1, axis=0)
    add_rows = jax.vmap(lambda values_block, index_list, extra: values_block.at[index_list].add(extra))
    result = add_rows(assembled[:, :owned_count], upper_lists, from_upper)
    result = add_rows(result, lower_lists, from_lower)
    return result.reshape(domains * owned_count, width) * inv_mass[:, None]


def reference(states, inv_mass, cell_ham, cell_nodes, send_up, send_down, owner, rotation_store):
    filtered_one = (sigma_one / filter_half) * (apply_operator(states, inv_mass, cell_ham, cell_nodes, send_up, send_down) - filter_center * states)
    applied = apply_operator(filtered_one, inv_mass, cell_ham, cell_nodes, send_up, send_down)
    filtered_two = (2.0 * sigma_two / filter_half) * (applied - filter_center * filtered_one) - sigma_one * sigma_two * states
    row_index = (owner[:, None] * PANEL_ROWS + jnp.arange(PANEL_ROWS, dtype=jnp.int32)[None, :]).reshape(-1).astype(jnp.int32)
    rotation = rotation_store[row_index]
    return jnp.dot(filtered_two, rotation, precision=lax.Precision.HIGHEST, preferred_element_type=jnp.float32)
```

```python
import math

import jax
import jax.numpy as jnp
from jax import lax
from jax.experimental import pallas as pl
from jax.experimental.pallas import tpu as pltpu
from jax.sharding import PartitionSpec as P

filter_center = 2.5
filter_half = 3.5
spectrum_floor = -4.0
sigma_one = filter_half / (spectrum_floor - filter_center)
sigma_two = 1.0 / (2.0 / sigma_one - sigma_one)
scale = 2.0 * sigma_one * sigma_two / filter_half**2
root_a = filter_center + filter_half / math.sqrt(2.0)
root_b = filter_center - filter_half / math.sqrt(2.0)

OWN = 192
GHOST = 48
COLS = 384
CELLS = 5
CN = 343
EXT = 320
FIRST = 128
PANEL = 24
STATES = 1536
HALF = OWN // 2

f32 = jnp.float32
bf16 = jnp.bfloat16


def split(x):
    high = x.astype(bf16)
    low = (x - high.astype(f32)).astype(bf16)
    return high, low


def dot(a, b):
    return jnp.dot(a, b, preferred_element_type=f32)


def mm2(pick, x):
    high, low = split(x)
    return dot(pick, high) + dot(pick, low)


def mm3(ah, al, bh, bl):
    return dot(ah, bh) + (dot(al, bh) + dot(ah, bl))


def column(row, count):
    wide = jnp.broadcast_to(row, (count, count))
    same = lax.broadcasted_iota(jnp.int32, (count, count), 0) == lax.broadcasted_iota(
        jnp.int32, (count, count), 1
    )
    return jnp.sum(jnp.where(same, wide, 0.0), axis=1, keepdims=True)


def one_hot(condition):
    return jnp.where(condition, 1.0, 0.0).astype(bf16)


def kernel(
    states, mass, ham, nodes, sup, sdn, owner, rot, out,
    xv, mv, hv, nv, upv, dnv, ownv, rb,
    gs, gr, rs, rr, amat, ah, al, fg, rh, rl, ov,
    ld, rsend, first_sem, second_sem, far_sem, mate_sem,
    gsend, grecv, bsend, brecv,
):
    d = lax.axis_index("dom")
    band = lax.axis_index("band")
    core = lax.rem(d, 2)
    y = lax.rem(d // 2, 4)
    zl = lax.rem(d // 8, 2)
    x = d // 16

    def dom_of(x_, y_, zl_, core_):
        return ((x_ * 2 + zl_) * 4 + y_) * 2 + core_

    def along_first(k):
        return dom_of(lax.rem(x + k * (1 - core), 4), lax.rem(y + k * core, 4), zl, core)

    def along_second(k):
        return dom_of(lax.rem(x + k * core, 4), lax.rem(y + k * (1 - core), 4), zl, core)

    f0 = x * (1 - core) + y * core
    s0 = y * (1 - core) + x * core

    def slot(s, f, z):
        return ((core * 4 + s) * 4 + f) * 2 + z

    up = (lax.rem(d + 1, 64), band)
    down = (lax.rem(d + 63, 64), band)
    f_up, f_down = (along_first(1), band), (along_first(3), band)
    s_up, s_down = (along_second(1), band), (along_second(3), band)
    z_mate = (dom_of(x, y, 1 - zl, core), band)
    mate = (dom_of(x, y, zl, 1 - core), band)
    b_up, b_down = (d, lax.rem(band + 1, 4)), (d, lax.rem(band + 3, 4))

    barrier = pltpu.get_barrier_semaphore()
    peers = (up, down, f_up, f_down, s_up, s_down, z_mate, mate, b_up, b_down)
    for peer in peers:
        pl.semaphore_signal(barrier, inc=1, device_id=peer, device_id_type=pl.DeviceIdType.MESH)

    def send(src, dst, ssem, rsem, peer):
        copy = pltpu.make_async_remote_copy(
            src_ref=src, dst_ref=dst, send_sem=ssem, recv_sem=rsem,
            device_id=peer, device_id_type=pl.DeviceIdType.MESH,
        )
        copy.start()
        return copy

    def arrived(dst, rsem):
        pltpu.make_async_copy(dst, dst, rsem).wait()

    my_columns = rot.at[:, pl.ds(pl.multiple_of(band * COLS, 128), COLS)]
    loads = [
        pltpu.make_async_copy(states, xv, ld.at[0]),
        pltpu.make_async_copy(mass, mv, ld.at[1]),
        pltpu.make_async_copy(sup, upv, ld.at[2]),
        pltpu.make_async_copy(sdn, dnv, ld.at[3]),
        pltpu.make_async_copy(nodes, nv, ld.at[4]),
        pltpu.make_async_copy(ham, hv, ld.at[5]),
        pltpu.make_async_copy(my_columns, rb.at[slot(s0, f0, zl)], ld.at[6]),
        pltpu.make_async_copy(owner, ownv, ld.at[7]),
    ]
    for load in loads:
        load.start()

    for load in loads[:4]:
        load.wait()
    up_row, down_row = upv[...], dnv[...]
    m = column(mv[...], OWN)
    lanes = lax.broadcasted_iota(jnp.int32, (GHOST, OWN), 1)
    pick_up = one_hot(column(up_row.astype(f32), GHOST).astype(jnp.int32) == lanes)
    pick_down = one_hot(column(down_row.astype(f32), GHOST).astype(jnp.int32) == lanes)
    rows = lax.broadcasted_iota(jnp.int32, (OWN, GHOST), 0)
    add_up = one_hot(rows == up_row)
    add_down = one_hot(rows == down_row)
    states_scaled = xv[...] * m

    def ghosts_out(k, values):
        high, low = split(values)
        gs[k, pl.ds(0, GHOST)] = dot(pick_up, high) + dot(pick_up, low)
        gs[k, pl.ds(GHOST, GHOST)] = dot(pick_down, high) + dot(pick_down, low)
        return [
            send(gs.at[k, pl.ds(0, GHOST)], gr.at[k, pl.ds(0, GHOST)],
                 gsend.at[k, 0], grecv.at[k, 0], up),
            send(gs.at[k, pl.ds(GHOST, GHOST)], gr.at[k, pl.ds(GHOST, GHOST)],
                 gsend.at[k, 1], grecv.at[k, 1], down),
        ]

    def apply_own(values):
        high, low = split(values)
        return mm3(ah[:, FIRST:], al[:, FIRST:], high, low)

    def ghosts_in(k):
        for side in range(2):
            part = gr.at[k, pl.ds(side * GHOST, GHOST)]
            arrived(part, grecv.at[k, side])
        high, low = split(gr[k])
        return mm3(ah[:, : 2 * GHOST], al[:, : 2 * GHOST], high, low)

    def sums_out(k, total):
        rs[k] = total[: 2 * GHOST]
        return [
            send(rs.at[k, pl.ds(0, GHOST)], rr.at[k, pl.ds(0, GHOST)],
                 gsend.at[k, 2], grecv.at[k, 2], down),
            send(rs.at[k, pl.ds(GHOST, GHOST)], rr.at[k, pl.ds(GHOST, GHOST)],
                 gsend.at[k, 3], grecv.at[k, 3], up),
        ]

    def sums_in(k):
        for side in range(2):
            arrived(rr.at[k, pl.ds(side * GHOST, GHOST)], grecv.at[k, 2 + side])
        return mm2(add_up, rr[k, pl.ds(0, GHOST)]) + mm2(add_down, rr[k, pl.ds(GHOST, GHOST)])

    pl.semaphore_wait(barrier, len(peers))

    sends = []
    sends += ghosts_out(0, states_scaled)

    sem = iter(range(64))

    def panel(src, s, f, z, rsem, peer):
        sends.append(send(src, rb.at[slot(s, f, z)], rsend.at[next(sem)], rsem, peer))

    def pair(s, f, rsem, peer):
        both = rb.at[pl.ds(slot(s, f, 0), 2)]
        sends.append(send(both, both, rsend.at[next(sem)], rsem, peer))

    def block(s):
        all_of = rb.at[pl.ds(slot(s, 0, 0), 8)]
        sends.append(send(all_of, all_of, rsend.at[next(sem)], mate_sem.at[s], mate))

    panel(my_columns, s0, f0, zl, first_sem.at[f0, zl], z_mate)
    panel(my_columns, s0, f0, zl, first_sem.at[f0, zl], f_up)
    panel(my_columns, s0, f0, zl, first_sem.at[f0, zl], f_down)

    f_next, f_last, f_far = lax.rem(f0 + 1, 4), lax.rem(f0 + 3, 4), lax.rem(f0 + 2, 4)
    s_next, s_last, s_far = lax.rem(s0 + 1, 4), lax.rem(s0 + 3, 4), lax.rem(s0 + 2, 4)

    def one_cell(c):
        node = nv[pl.ds(c, 1)]
        where = jnp.where(node < OWN, node + FIRST, node - OWN)
        place = one_hot(lax.broadcasted_iota(jnp.int32, (EXT, CN), 0) == where)
        high, low = split(hv[c])
        nt = (((1,), (1,)), ((), ()))
        half = lax.dot_general(high, place, nt, preferred_element_type=f32)
        half = half + lax.dot_general(low, place, nt, preferred_element_type=f32)
        total = mm2(place, half)
        if c == 0:
            amat[...] = total
        else:
            amat[...] += total

    loads[4].wait()
    loads[5].wait()
    one_cell(0)
    loads[6].wait()

    one_cell(1)
    other = 1 - zl
    arrived(rb.at[slot(s0, f0, other)], first_sem.at[f0, other])
    panel(rb.at[slot(s0, f0, other)], s0, f0, other, first_sem.at[f0, other], f_up)
    panel(rb.at[slot(s0, f0, other)], s0, f0, other, first_sem.at[f0, other], f_down)
    pair(s0, f0, second_sem.at[s0, f0], s_up)
    pair(s0, f0, second_sem.at[s0, f0], s_down)
    one_cell(2)
    one_cell(3)

    arrived(rb.at[slot(s0, f_last, 0)], first_sem.at[f_last, 0])
    panel(rb.at[slot(s0, f_last, 0)], s0, f_last, 0, first_sem.at[f_last, 0], f_up)
    arrived(rb.at[slot(s0, f_next, 1)], first_sem.at[f_next, 1])
    panel(rb.at[slot(s0, f_next, 1)], s0, f_next, 1, first_sem.at[f_next, 1], f_down)
    arrived(rb.at[slot(s0, f_last, 1)], first_sem.at[f_last, 1])
    pair(s0, f_last, second_sem.at[s0, f_last], s_up)
    pair(s0, f_last, second_sem.at[s0, f_last], s_down)
    arrived(rb.at[slot(s0, f_next, 0)], first_sem.at[f_next, 0])
    pair(s0, f_next, second_sem.at[s0, f_next], s_up)
    pair(s0, f_next, second_sem.at[s0, f_next], s_down)

    one_cell(4)
    ahv, alv = split(amat[...])
    ah[...] = ahv
    al[...] = alv
    total = apply_own(states_scaled)
    total = total + ghosts_in(0)
    sends += sums_out(0, total)

    def relay(f):
        arrived(rb.at[pl.ds(slot(s_last, f, 0), 2)], second_sem.at[s_last, f])
        panel(rb.at[slot(s_last, f, 0)], s_last, f, 0, far_sem.at[f, 0], s_up)
        arrived(rb.at[pl.ds(slot(s_next, f, 0), 2)], second_sem.at[s_next, f])
        panel(rb.at[slot(s_next, f, 1)], s_next, f, 1, far_sem.at[f, 1], s_down)

    for z in range(2):
        arrived(rb.at[slot(s0, f_far, z)], first_sem.at[f_far, z])
    pair(s0, f_far, second_sem.at[s0, f_far], s_up)
    pair(s0, f_far, second_sem.at[s0, f_far], s_down)
    block(s0)
    relay(f0)
    relay(f_last)
    relay(f_next)

    step = m * (total[FIRST:] + sums_in(0)) - root_a * xv[...]
    step_scaled = step * m
    sends += ghosts_out(1, step_scaled)
    relay(f_far)
    block(s_last)
    block(s_next)
    total = apply_own(step_scaled)
    total = total + ghosts_in(1)
    sends += sums_out(1, total)
    for f in (f0, f_last, f_next, f_far):
        for z in range(2):
            arrived(rb.at[slot(s_far, f, z)], far_sem.at[f, z])
    block(s_far)

    mate_s0 = s0 * 0 + f0
    for k in (0, 3, 1, 2):
        s = lax.rem(mate_s0 + k, 4)
        theirs = rb.at[pl.ds((((1 - core) * 4 + s) * 4) * 2, 8)]
        arrived(theirs, mate_sem.at[s])
    loads[7].wait()

    def place_of(p):
        o = ownv[p]
        c_, y_, z_, x_ = lax.rem(o, 2), lax.rem(o // 2, 4), lax.rem(o // 8, 2), o // 16
        f_, s_ = x_ * (1 - c_) + y_ * c_, y_ * (1 - c_) + x_ * c_
        return ((c_ * 4 + s_) * 4 + f_) * 2 + z_

    def reorder(q, carry):
        two = jnp.concatenate([rb[place_of(2 * q)], rb[place_of(2 * q + 1)]], axis=0)
        high, low = split(two)
        at = pl.ds(pl.multiple_of(q * 2 * PANEL, 16), 2 * PANEL)
        rh[at] = high
        rl[at] = low
        return carry

    lax.fori_loop(0, STATES // (2 * PANEL), reorder, 0)

    result = scale * (m * (total[FIRST:] + sums_in(1)) - root_b * step)
    fg[band] = result

    b_next, b_last, b_far = lax.rem(band + 1, 4), lax.rem(band + 3, 4), lax.rem(band + 2, 4)
    bs = iter(range(6))

    def rows_to(b, h, peer):
        part = fg.at[b, pl.ds(h * HALF, HALF)]
        sends.append(send(part, part, bsend.at[next(bs)], brecv.at[b, h], peer))

    rows_to(band, 0, b_up)
    rows_to(band, 1, b_down)
    rows_to(band, 1, b_up)
    rows_to(band, 0, b_down)

    def times(values, b):
        high, low = split(values)
        at = pl.ds(pl.multiple_of(b * COLS, 128), COLS)
        return mm3(high, low, rh[at], rl[at])

    def got(b, h):
        arrived(fg.at[b, pl.ds(h * HALF, HALF)], brecv.at[b, h])

    ov[...] = times(result, band)
    got(b_last, 0)
    rows_to(b_last, 0, b_up)
    got(b_next, 1)
    rows_to(b_next, 1, b_down)
    top, bottom = pl.ds(0, HALF), pl.ds(HALF, HALF)
    ov[top] += times(fg[b_last, top], b_last)
    ov[bottom] += times(fg[b_next, bottom], b_next)
    got(b_last, 1)
    ov[bottom] += times(fg[b_last, bottom], b_last)
    got(b_next, 0)
    ov[top] += times(fg[b_next, top], b_next)
    got(b_far, 0)
    ov[top] += times(fg[b_far, top], b_far)
    got(b_far, 1)
    ov[bottom] += times(fg[b_far, bottom], b_far)

    store = pltpu.make_async_copy(ov, out, ld.at[0])
    store.start()
    for copy in sends:
        copy.wait_send()
    store.wait()


def shards(states, inv_mass, cell_ham, cell_nodes, send_up, send_down, owner, rotation_store):
    dma = pltpu.SemaphoreType.DMA
    vmem = pltpu.VMEM
    return pl.pallas_call(
        kernel,
        out_shape=jax.ShapeDtypeStruct((OWN, COLS), f32),
        in_specs=[pl.BlockSpec(memory_space=pl.ANY)] * 8,
        out_specs=pl.BlockSpec(memory_space=pl.ANY),
        scratch_shapes=[
            vmem((OWN, COLS), f32),
            vmem((1, OWN), f32),
            vmem((CELLS, CN, CN), f32),
            vmem((CELLS, CN), jnp.int32),
            vmem((1, GHOST), jnp.int32),
            vmem((1, GHOST), jnp.int32),
            pltpu.SMEM((64,), jnp.int32),
            vmem((64, PANEL, COLS), f32),
            vmem((2, 2 * GHOST, COLS), f32),
            vmem((2, 2 * GHOST, COLS), f32),
            vmem((2, 2 * GHOST, COLS), f32),
            vmem((2, 2 * GHOST, COLS), f32),
            vmem((EXT, EXT), f32),
            vmem((EXT, EXT), bf16),
            vmem((EXT, EXT), bf16),
            vmem((4, OWN, COLS), f32),
            vmem((STATES, COLS), bf16),
            vmem((STATES, COLS), bf16),
            vmem((OWN, COLS), f32),
            dma((8,)),
            dma((64,)),
            dma((4, 2)),
            dma((4, 4)),
            dma((4, 2)),
            dma((4,)),
            dma((2, 4)),
            dma((2, 4)),
            dma((6,)),
            dma((4, 2)),
        ],
        compiler_params=pltpu.CompilerParams(
            collective_id=0, has_side_effects=True, vmem_limit_bytes=56 * 1024 * 1024
        ),
    )(
        states,
        inv_mass.reshape(1, OWN),
        cell_ham,
        cell_nodes,
        send_up.reshape(1, GHOST),
        send_down.reshape(1, GHOST),
        owner,
        rotation_store,
    )


def solution(mesh):
    in_specs = (
        P("dom", "band"),
        P("dom"),
        P("dom", None, None),
        P("dom", None),
        P("dom"),
        P("dom"),
        P(),
        P("dom", None),
    )
    return jax.shard_map(
        shards, mesh=mesh, in_specs=in_specs, out_specs=P("dom", "band"), check_vma=False
    )
```

```python
import math

import jax
import jax.numpy as jnp
from jax import lax
from jax.experimental import pallas as pl
from jax.experimental.pallas import tpu as pltpu
from jax.sharding import PartitionSpec as P

filter_center = 2.5
filter_half = 3.5
spectrum_floor = -4.0
sigma_one = filter_half / (spectrum_floor - filter_center)
sigma_two = 1.0 / (2.0 / sigma_one - sigma_one)
scale = 2.0 * sigma_one * sigma_two / filter_half**2
root_a = filter_center + filter_half / math.sqrt(2.0)
root_b = filter_center - filter_half / math.sqrt(2.0)

OWN = 192
GHOST = 48
COLS = 384
CELLS = 5
CN = 343
EXT = 320
FIRST = 128
PANEL = 24
STATES = 1536
HALF = OWN // 2
EARLY = 128
LATE = COLS - EARLY

f32 = jnp.float32
bf16 = jnp.bfloat16


def split(x):
    high = x.astype(bf16)
    low = (x - high.astype(f32)).astype(bf16)
    return high, low


def dot(a, b):
    return jnp.dot(a, b, preferred_element_type=f32)


def mm2(pick, x):
    high, low = split(x)
    return dot(pick, high) + dot(pick, low)


def mm3(ah, al, bh, bl):
    return dot(ah, bh) + (dot(al, bh) + dot(ah, bl))


def column(row, count):
    wide = jnp.broadcast_to(row, (count, count))
    same = lax.broadcasted_iota(jnp.int32, (count, count), 0) == lax.broadcasted_iota(
        jnp.int32, (count, count), 1
    )
    return jnp.sum(jnp.where(same, wide, 0.0), axis=1, keepdims=True)


def one_hot(condition):
    return jnp.where(condition, 1.0, 0.0).astype(bf16)


def kernel(
    states, mass, ham, nodes, sup, sdn, owner, rot, out,
    xv, mv, hv, nv, upv, dnv, ownv, rb,
    gs0, gr0, rs0, rr0, gs1, gr1, rs1, rr1, gs2, gr2, rs2, rr2,
    amat, ah, al, fe, fl, rh, rl, ov,
    ld, psend, first_sem, second_sem, mate_sem,
    gsend, grecv, bsend, erecv, lrecv,
):
    d = lax.axis_index("dom")
    band = lax.axis_index("band")
    core = lax.rem(d, 2)
    y = lax.rem(d // 2, 4)
    zl = lax.rem(d // 8, 2)
    x = d // 16
    other = 1 - zl

    def dom_of(x_, y_, zl_, core_):
        return ((x_ * 2 + zl_) * 4 + y_) * 2 + core_

    def along_first(k, z):
        return dom_of(lax.rem(x + k * (1 - core), 4), lax.rem(y + k * core, 4), z, core), band

    def along_second(k):
        return dom_of(lax.rem(x + k * core, 4), lax.rem(y + k * (1 - core), 4), zl, core), band

    f0 = x * (1 - core) + y * core
    s0 = y * (1 - core) + x * core

    def slot(c, s, f, z):
        return ((c * 4 + s) * 4 + f) * 2 + z

    up = (lax.rem(d + 1, 64), band)
    down = (lax.rem(d + 63, 64), band)
    mate = (dom_of(x, y, zl, 1 - core), band)
    b_up, b_down = (d, lax.rem(band + 1, 4)), (d, lax.rem(band + 3, 4))
    firsts = [along_first(k, zl) for k in (1, 3, 2)] + [along_first(k, other) for k in (0, 1, 3, 2)]
    seconds = [along_second(k) for k in (1, 3, 2)]

    barrier = pltpu.get_barrier_semaphore()
    peers = [up, down, mate, b_up, b_down] + firsts + seconds
    for peer in peers:
        pl.semaphore_signal(barrier, inc=1, device_id=peer, device_id_type=pl.DeviceIdType.MESH)

    sends = []

    def send(src, dst, ssem, rsem, peer):
        copy = pltpu.make_async_remote_copy(
            src_ref=src, dst_ref=dst, send_sem=ssem, recv_sem=rsem,
            device_id=peer, device_id_type=pl.DeviceIdType.MESH,
        )
        copy.start()
        sends.append(copy)

    def arrived(dst, rsem):
        pltpu.make_async_copy(dst, dst, rsem).wait()

    my_columns = rot.at[:, pl.ds(pl.multiple_of(band * COLS, 128), COLS)]
    loads = [
        pltpu.make_async_copy(states, xv, ld.at[0]),
        pltpu.make_async_copy(mass, mv, ld.at[1]),
        pltpu.make_async_copy(sup, upv, ld.at[2]),
        pltpu.make_async_copy(sdn, dnv, ld.at[3]),
        pltpu.make_async_copy(nodes, nv, ld.at[4]),
        pltpu.make_async_copy(ham, hv, ld.at[5]),
        pltpu.make_async_copy(my_columns, rb.at[slot(core, s0, f0, zl)], ld.at[6]),
        pltpu.make_async_copy(owner, ownv, ld.at[7]),
    ]
    for load in loads:
        load.start()

    for load in loads[:4]:
        load.wait()
    up_row, down_row = upv[...], dnv[...]
    m = column(mv[...], OWN)
    lanes = lax.broadcasted_iota(jnp.int32, (GHOST, OWN), 1)
    pick_up = one_hot(column(up_row.astype(f32), GHOST).astype(jnp.int32) == lanes)
    pick_down = one_hot(column(down_row.astype(f32), GHOST).astype(jnp.int32) == lanes)
    rows = lax.broadcasted_iota(jnp.int32, (OWN, GHOST), 0)
    add_up = one_hot(rows == up_row)
    add_down = one_hot(rows == down_row)
    states_scaled = xv[...] * m
    low_part, high_part = pl.ds(0, GHOST), pl.ds(GHOST, GHOST)
    ghost_send, ghost_recv = (gs0, gs1, gs2), (gr0, gr1, gr2)
    sum_send, sum_recv = (rs0, rs1, rs2), (rr0, rr1, rr2)

    def ghosts_out(k, values):
        src, dst = ghost_send[k], ghost_recv[k]
        high, low = split(values)
        src[low_part] = dot(pick_up, high) + dot(pick_up, low)
        send(src.at[low_part], dst.at[low_part], gsend.at[k, 0], grecv.at[k, 0], up)
        src[high_part] = dot(pick_down, high) + dot(pick_down, low)
        send(src.at[high_part], dst.at[high_part], gsend.at[k, 1], grecv.at[k, 1], down)

    def apply_own(values):
        high, low = split(values)
        return mm3(ah[:, FIRST:], al[:, FIRST:], high, low)

    def ghosts_in(k):
        arrived(ghost_recv[k].at[low_part], grecv.at[k, 0])
        arrived(ghost_recv[k].at[high_part], grecv.at[k, 1])
        high, low = split(ghost_recv[k][...])
        return mm3(ah[:, : 2 * GHOST], al[:, : 2 * GHOST], high, low)

    def sums_out(k, total):
        src, dst = sum_send[k], sum_recv[k]
        src[...] = total[: 2 * GHOST]
        send(src.at[low_part], dst.at[low_part], gsend.at[k, 2], grecv.at[k, 2], down)
        send(src.at[high_part], dst.at[high_part], gsend.at[k, 3], grecv.at[k, 3], up)

    def sums_in(k):
        arrived(sum_recv[k].at[low_part], grecv.at[k, 2])
        arrived(sum_recv[k].at[high_part], grecv.at[k, 3])
        return mm2(add_up, sum_recv[k][low_part]) + mm2(add_down, sum_recv[k][high_part])

    def one_cell(c):
        node = nv[pl.ds(c, 1)]
        where = jnp.where(node < OWN, node + FIRST, node - OWN)
        place = one_hot(lax.broadcasted_iota(jnp.int32, (EXT, CN), 0) == where)
        high, low = split(hv[c])
        nt = (((1,), (1,)), ((), ()))
        half = lax.dot_general(high, place, nt, preferred_element_type=f32)
        half = half + lax.dot_general(low, place, nt, preferred_element_type=f32)
        total = mm2(place, half)
        if c == 0:
            amat[...] = total
        else:
            amat[...] += total

    pl.semaphore_wait(barrier, len(peers))

    ghosts_out(0, states_scaled)

    number = iter(range(32))
    for peer in firsts:
        send(my_columns, rb.at[slot(core, s0, f0, zl)], psend.at[next(number)], first_sem.at[f0, zl], peer)

    def four(c, s, h):
        return rb.at[pl.ds(slot(c, s, 2 * h, 0), 4)]

    def spread(h):
        for peer in seconds:
            send(four(core, s0, h), four(core, s0, h), psend.at[next(number)], second_sem.at[s0, h], peer)

    def pass_on(s, h):
        send(four(core, s, h), four(core, s, h), psend.at[next(number)], mate_sem.at[s, h], mate)

    loads[4].wait()
    loads[5].wait()
    for c in range(CELLS):
        one_cell(c)
    ahv, alv = split(amat[...])
    ah[...] = ahv
    al[...] = alv
    total = apply_own(states_scaled)
    total = total + ghosts_in(0)
    sums_out(0, total)

    for k in (1, 3, 2):
        f = lax.rem(f0 + k, 4)
        arrived(rb.at[slot(core, s0, f, zl)], first_sem.at[f, zl])
    for k in (0, 1, 3, 2):
        f = lax.rem(f0 + k, 4)
        arrived(rb.at[slot(core, s0, f, other)], first_sem.at[f, other])
    loads[6].wait()
    spread(0)
    pass_on(s0, 0)
    pass_on(s0, 1)

    b_next, b_last, b_far = lax.rem(band + 1, 4), lax.rem(band + 3, 4), lax.rem(band + 2, 4)
    bnumber = iter(range(12))
    top, bottom = pl.ds(0, HALF), pl.ds(HALF, HALF)
    halves = (top, bottom)

    def rows_to(buf, recv, b, h, peer):
        part = buf.at[b, halves[h]]
        send(part, part, bsend.at[next(bnumber)], recv.at[b, h], peer)

    def over_band(buf, recv):
        rows_to(buf, recv, band, 0, b_up)
        rows_to(buf, recv, band, 1, b_down)
        rows_to(buf, recv, band, 1, b_up)
        rows_to(buf, recv, band, 0, b_down)

    def got(buf, recv, b, h):
        arrived(buf.at[b, halves[h]], recv.at[b, h])

    def relay(buf, recv):
        got(buf, recv, b_last, 0)
        rows_to(buf, recv, b_last, 0, b_up)
        got(buf, recv, b_next, 1)
        rows_to(buf, recv, b_next, 1, b_down)

    step = m * (total[FIRST:] + sums_in(0)) - root_a * xv[...]
    fe[band] = step[:, :EARLY]
    over_band(fe, erecv)
    late = step[:, EARLY:]
    late_scaled = late * m
    ghosts_out(1, late_scaled)
    spread(1)
    total = apply_own(late_scaled)
    relay(fe, erecv)
    total = total + ghosts_in(1)
    sums_out(1, total)

    for h in range(2):
        for k in (1, 3, 2):
            s = lax.rem(s0 + k, 4)
            arrived(four(core, s, h), second_sem.at[s, h])
            pass_on(s, h)

    late = scale * (m * (total[FIRST:] + sums_in(1)) - root_b * late)
    fl[band] = late
    over_band(fl, lrecv)

    for k in (0, 1, 3, 2):
        s = lax.rem(f0 + k, 4)
        for h in range(2):
            arrived(four(1 - core, s, h), mate_sem.at[s, h])
    loads[7].wait()

    def place_of(p):
        o = ownv[p]
        c_, y_, z_, x_ = lax.rem(o, 2), lax.rem(o // 2, 4), lax.rem(o // 8, 2), o // 16
        f_, s_ = x_ * (1 - c_) + y_ * c_, y_ * (1 - c_) + x_ * c_
        return slot(c_, s_, f_, z_)

    def reorder(q, carry):
        two = jnp.concatenate([rb[place_of(2 * q)], rb[place_of(2 * q + 1)]], axis=0)
        high, low = split(two)
        at = pl.ds(pl.multiple_of(q * 2 * PANEL, 16), 2 * PANEL)
        rh[at] = high
        rl[at] = low
        return carry

    lax.fori_loop(0, STATES // (2 * PANEL), reorder, 0)

    def times(values, b, first, count):
        high, low = split(values)
        at = pl.ds(pl.multiple_of(b * COLS + first, 128), count)
        return mm3(high, low, rh[at], rl[at])

    got(fe, erecv, b_last, 1)
    got(fe, erecv, b_next, 0)
    got(fe, erecv, b_far, 0)
    got(fe, erecv, b_far, 1)
    turned = times(fe[0], 0, 0, EARLY) + times(fe[1], 1, 0, EARLY)
    turned = turned + (times(fe[2], 2, 0, EARLY) + times(fe[3], 3, 0, EARLY))
    turned_scaled = turned * m
    ghosts_out(2, turned_scaled)
    total = apply_own(turned_scaled)
    relay(fl, lrecv)
    ov[...] = times(late, band, EARLY, LATE)
    ov[top] += times(fl[b_last, top], b_last, EARLY, LATE)
    ov[bottom] += times(fl[b_next, bottom], b_next, EARLY, LATE)
    total = total + ghosts_in(2)
    sums_out(2, total)
    got(fl, lrecv, b_last, 1)
    ov[bottom] += times(fl[b_last, bottom], b_last, EARLY, LATE)
    got(fl, lrecv, b_next, 0)
    ov[top] += times(fl[b_next, top], b_next, EARLY, LATE)
    ov[...] += scale * (m * (total[FIRST:] + sums_in(2)) - root_b * turned)
    got(fl, lrecv, b_far, 0)
    ov[top] += times(fl[b_far, top], b_far, EARLY, LATE)
    got(fl, lrecv, b_far, 1)
    ov[bottom] += times(fl[b_far, bottom], b_far, EARLY, LATE)

    store = pltpu.make_async_copy(ov, out, ld.at[0])
    store.start()
    for copy in sends:
        copy.wait_send()
    store.wait()


def shards(states, inv_mass, cell_ham, cell_nodes, send_up, send_down, owner, rotation_store):
    dma = pltpu.SemaphoreType.DMA
    vmem = pltpu.VMEM
    edges = [vmem((2 * GHOST, n), f32) for n in (COLS, LATE, COLS) for _ in range(4)]
    return pl.pallas_call(
        kernel,
        out_shape=jax.ShapeDtypeStruct((OWN, COLS), f32),
        in_specs=[pl.BlockSpec(memory_space=pl.ANY)] * 8,
        out_specs=pl.BlockSpec(memory_space=pl.ANY),
        scratch_shapes=[
            vmem((OWN, COLS), f32),
            vmem((1, OWN), f32),
            vmem((CELLS, CN, CN), f32),
            vmem((CELLS, CN), jnp.int32),
            vmem((1, GHOST), jnp.int32),
            vmem((1, GHOST), jnp.int32),
            pltpu.SMEM((64,), jnp.int32),
            vmem((64, PANEL, COLS), f32),
            *edges,
            vmem((EXT, EXT), f32),
            vmem((EXT, EXT), bf16),
            vmem((EXT, EXT), bf16),
            vmem((4, OWN, EARLY), f32),
            vmem((4, OWN, LATE), f32),
            vmem((STATES, COLS), bf16),
            vmem((STATES, COLS), bf16),
            vmem((OWN, COLS), f32),
            dma((8,)),
            dma((32,)),
            dma((4, 2)),
            dma((4, 2)),
            dma((4, 2)),
            dma((3, 4)),
            dma((3, 4)),
            dma((12,)),
            dma((4, 2)),
            dma((4, 2)),
        ],
        compiler_params=pltpu.CompilerParams(
            collective_id=0, has_side_effects=True, vmem_limit_bytes=56 * 1024 * 1024
        ),
    )(
        states,
        inv_mass.reshape(1, OWN),
        cell_ham,
        cell_nodes,
        send_up.reshape(1, GHOST),
        send_down.reshape(1, GHOST),
        owner,
        rotation_store,
    )


def solution(mesh):
    in_specs = (
        P("dom", "band"),
        P("dom"),
        P("dom", None, None),
        P("dom", None),
        P("dom"),
        P("dom"),
        P(),
        P("dom", None),
    )
    return jax.shard_map(
        shards, mesh=mesh, in_specs=in_specs, out_specs=P("dom", "band"), check_vma=False
    )
```

```python
import math

import jax
import jax.numpy as jnp
from jax import lax
from jax.experimental import pallas as pl
from jax.experimental.pallas import tpu as pltpu
from jax.sharding import PartitionSpec as P

filter_center = 2.5
filter_half = 3.5
spectrum_floor = -4.0
sigma_one = filter_half / (spectrum_floor - filter_center)
sigma_two = 1.0 / (2.0 / sigma_one - sigma_one)
scale = 2.0 * sigma_one * sigma_two / filter_half**2
root_a = filter_center + filter_half / math.sqrt(2.0)
root_b = filter_center - filter_half / math.sqrt(2.0)

OWN = 192
GHOST = 48
COLS = 384
CELLS = 5
CN = 343
EXT = 320
FIRST = 128
PANEL = 24
STATES = 1536
HALF = OWN // 2
EARLY = 128
LATE = COLS - EARLY

f32 = jnp.float32
bf16 = jnp.bfloat16


def split(x):
    high = x.astype(bf16)
    low = (x - high.astype(f32)).astype(bf16)
    return high, low


def dot(a, b):
    return jnp.dot(a, b, preferred_element_type=f32)


def mm2(pick, x):
    high, low = split(x)
    return dot(pick, high) + dot(pick, low)


def mm3(ah, al, bh, bl):
    return dot(ah, bh) + (dot(al, bh) + dot(ah, bl))


def column(row, count):
    wide = jnp.broadcast_to(row, (count, count))
    same = lax.broadcasted_iota(jnp.int32, (count, count), 0) == lax.broadcasted_iota(
        jnp.int32, (count, count), 1
    )
    return jnp.sum(jnp.where(same, wide, 0.0), axis=1, keepdims=True)


def one_hot(condition):
    return jnp.where(condition, 1.0, 0.0).astype(bf16)


def kernel(
    states, mass, ham, nodes, sup, sdn, owner, rot, ov,
    xv, mv, hv, nv, upv, dnv, ownv, rb,
    gs0, gr0, rs0, rr0, gs1, gr1, rs1, rr1, gs2, gr2, rs2, rr2,
    amat, ah, al, fe, fl, rh, rl,
    ld, psend, first_sem, second_sem, mate_sem,
    gsend, grecv, bsend, erecv, lrecv,
):
    d = lax.axis_index("dom")
    band = lax.axis_index("band")
    core = lax.rem(d, 2)
    y = lax.rem(d // 2, 4)
    zl = lax.rem(d // 8, 2)
    x = d // 16
    other = 1 - zl

    def dom_of(x_, y_, zl_, core_):
        return ((x_ * 2 + zl_) * 4 + y_) * 2 + core_

    def along_first(k, z):
        return dom_of(lax.rem(x + k * (1 - core), 4), lax.rem(y + k * core, 4), z, core), band

    def along_second(k):
        return dom_of(lax.rem(x + k * core, 4), lax.rem(y + k * (1 - core), 4), zl, core), band

    f0 = x * (1 - core) + y * core
    s0 = y * (1 - core) + x * core

    def slot(c, s, f, z):
        return ((c * 4 + s) * 4 + f) * 2 + z

    up = (lax.rem(d + 1, 64), band)
    down = (lax.rem(d + 63, 64), band)
    mate = (dom_of(x, y, zl, 1 - core), band)
    b_up, b_down = (d, lax.rem(band + 1, 4)), (d, lax.rem(band + 3, 4))
    firsts = [along_first(k, zl) for k in (1, 3, 2)] + [along_first(k, other) for k in (0, 1, 3, 2)]
    seconds = [along_second(k) for k in (1, 3, 2)]

    barrier = pltpu.get_barrier_semaphore()
    peers = [up, down, mate, b_up, b_down] + firsts + seconds
    for peer in peers:
        pl.semaphore_signal(barrier, inc=1, device_id=peer, device_id_type=pl.DeviceIdType.MESH)

    sends = []

    def send(src, dst, ssem, rsem, peer):
        copy = pltpu.make_async_remote_copy(
            src_ref=src, dst_ref=dst, send_sem=ssem, recv_sem=rsem,
            device_id=peer, device_id_type=pl.DeviceIdType.MESH,
        )
        copy.start()
        sends.append(copy)

    def arrived(dst, rsem):
        pltpu.make_async_copy(dst, dst, rsem).wait()

    my_columns = rot.at[:, pl.ds(pl.multiple_of(band * COLS, 128), COLS)]
    loads = [
        pltpu.make_async_copy(states, xv, ld.at[0]),
        pltpu.make_async_copy(mass, mv, ld.at[1]),
        pltpu.make_async_copy(sup, upv, ld.at[2]),
        pltpu.make_async_copy(sdn, dnv, ld.at[3]),
        pltpu.make_async_copy(nodes, nv, ld.at[4]),
        pltpu.make_async_copy(ham, hv, ld.at[5]),
        pltpu.make_async_copy(my_columns, rb.at[slot(core, s0, f0, zl)], ld.at[6]),
        pltpu.make_async_copy(owner, ownv, ld.at[7]),
    ]
    for load in loads:
        load.start()

    for load in loads[:4]:
        load.wait()
    up_row, down_row = upv[...], dnv[...]
    m = column(mv[...], OWN)
    lanes = lax.broadcasted_iota(jnp.int32, (GHOST, OWN), 1)
    pick_up = one_hot(column(up_row.astype(f32), GHOST).astype(jnp.int32) == lanes)
    pick_down = one_hot(column(down_row.astype(f32), GHOST).astype(jnp.int32) == lanes)
    rows = lax.broadcasted_iota(jnp.int32, (OWN, GHOST), 0)
    add_up = one_hot(rows == up_row)
    add_down = one_hot(rows == down_row)
    states_scaled = xv[...] * m
    low_part, high_part = pl.ds(0, GHOST), pl.ds(GHOST, GHOST)
    ghost_send, ghost_recv = (gs0, gs1, gs2), (gr0, gr1, gr2)
    sum_send, sum_recv = (rs0, rs1, rs2), (rr0, rr1, rr2)

    def ghosts_out(k, values):
        src, dst = ghost_send[k], ghost_recv[k]
        high, low = split(values)
        src[low_part] = dot(pick_up, high) + dot(pick_up, low)
        send(src.at[low_part], dst.at[low_part], gsend.at[k, 0], grecv.at[k, 0], up)
        src[high_part] = dot(pick_down, high) + dot(pick_down, low)
        send(src.at[high_part], dst.at[high_part], gsend.at[k, 1], grecv.at[k, 1], down)

    def apply_own(values):
        high, low = split(values)
        return mm3(ah[:, FIRST:], al[:, FIRST:], high, low)

    def ghosts_in(k):
        arrived(ghost_recv[k].at[low_part], grecv.at[k, 0])
        arrived(ghost_recv[k].at[high_part], grecv.at[k, 1])
        high, low = split(ghost_recv[k][...])
        return mm3(ah[:, : 2 * GHOST], al[:, : 2 * GHOST], high, low)

    def sums_out(k, total):
        src, dst = sum_send[k], sum_recv[k]
        src[...] = total[: 2 * GHOST]
        send(src.at[low_part], dst.at[low_part], gsend.at[k, 2], grecv.at[k, 2], down)
        send(src.at[high_part], dst.at[high_part], gsend.at[k, 3], grecv.at[k, 3], up)

    def sums_in(k):
        arrived(sum_recv[k].at[low_part], grecv.at[k, 2])
        arrived(sum_recv[k].at[high_part], grecv.at[k, 3])
        return mm2(add_up, sum_recv[k][low_part]) + mm2(add_down, sum_recv[k][high_part])

    def one_cell(c):
        node = nv[pl.ds(c, 1)]
        where = jnp.where(node < OWN, node + FIRST, node - OWN)
        place = one_hot(lax.broadcasted_iota(jnp.int32, (EXT, CN), 0) == where)
        high, low = split(hv[c])
        nt = (((1,), (1,)), ((), ()))
        half = lax.dot_general(high, place, nt, preferred_element_type=f32)
        half = half + lax.dot_general(low, place, nt, preferred_element_type=f32)
        total = mm2(place, half)
        if c == 0:
            amat[...] = total
        else:
            amat[...] += total

    pl.semaphore_wait(barrier, len(peers))

    ghosts_out(0, states_scaled)

    number = iter(range(32))
    for peer in firsts:
        send(my_columns, rb.at[slot(core, s0, f0, zl)], psend.at[next(number)], first_sem.at[f0, zl], peer)

    def four(c, s, h):
        return rb.at[pl.ds(slot(c, s, 2 * h, 0), 4)]

    def spread(h):
        for peer in seconds:
            send(four(core, s0, h), four(core, s0, h), psend.at[next(number)], second_sem.at[s0, h], peer)

    def pass_on(s, h):
        send(four(core, s, h), four(core, s, h), psend.at[next(number)], mate_sem.at[s, h], mate)

    loads[4].wait()
    loads[5].wait()
    for c in range(CELLS):
        one_cell(c)
    ahv, alv = split(amat[...])
    ah[...] = ahv
    al[...] = alv
    total = apply_own(states_scaled)
    total = total + ghosts_in(0)
    sums_out(0, total)

    for k in (1, 3, 2):
        f = lax.rem(f0 + k, 4)
        arrived(rb.at[slot(core, s0, f, zl)], first_sem.at[f, zl])
    for k in (0, 1, 3, 2):
        f = lax.rem(f0 + k, 4)
        arrived(rb.at[slot(core, s0, f, other)], first_sem.at[f, other])
    loads[6].wait()
    spread(0)
    pass_on(s0, 0)
    pass_on(s0, 1)

    b_next, b_last, b_far = lax.rem(band + 1, 4), lax.rem(band + 3, 4), lax.rem(band + 2, 4)
    bnumber = iter(range(12))
    top, bottom = pl.ds(0, HALF), pl.ds(HALF, HALF)
    halves = (top, bottom)

    def rows_to(buf, recv, b, h, peer):
        part = buf.at[b, halves[h]]
        send(part, part, bsend.at[next(bnumber)], recv.at[b, h], peer)

    def over_band(buf, recv):
        rows_to(buf, recv, band, 0, b_up)
        rows_to(buf, recv, band, 1, b_down)
        rows_to(buf, recv, band, 1, b_up)
        rows_to(buf, recv, band, 0, b_down)

    def got(buf, recv, b, h):
        arrived(buf.at[b, halves[h]], recv.at[b, h])

    def relay(buf, recv):
        got(buf, recv, b_last, 0)
        rows_to(buf, recv, b_last, 0, b_up)
        got(buf, recv, b_next, 1)
        rows_to(buf, recv, b_next, 1, b_down)

    step = m * (total[FIRST:] + sums_in(0)) - root_a * xv[...]
    fe[band] = step[:, :EARLY]
    over_band(fe, erecv)
    late = step[:, EARLY:]
    late_scaled = late * m
    ghosts_out(1, late_scaled)
    spread(1)
    total = apply_own(late_scaled)
    relay(fe, erecv)
    total = total + ghosts_in(1)
    sums_out(1, total)

    for h in range(2):
        for k in (1, 3, 2):
            s = lax.rem(s0 + k, 4)
            arrived(four(core, s, h), second_sem.at[s, h])
            pass_on(s, h)

    late = scale * (m * (total[FIRST:] + sums_in(1)) - root_b * late)
    fl[band] = late
    over_band(fl, lrecv)

    for k in (0, 1, 3, 2):
        s = lax.rem(f0 + k, 4)
        for h in range(2):
            arrived(four(1 - core, s, h), mate_sem.at[s, h])
    loads[7].wait()

    def place_of(p):
        o = ownv[p]
        c_, y_, z_, x_ = lax.rem(o, 2), lax.rem(o // 2, 4), lax.rem(o // 8, 2), o // 16
        f_, s_ = x_ * (1 - c_) + y_ * c_, y_ * (1 - c_) + x_ * c_
        return slot(c_, s_, f_, z_)

    def reorder(q, carry):
        two = jnp.concatenate([rb[place_of(2 * q)], rb[place_of(2 * q + 1)]], axis=0)
        high, low = split(two)
        at = pl.ds(pl.multiple_of(q * 2 * PANEL, 16), 2 * PANEL)
        rh[at] = high
        rl[at] = low
        return carry

    lax.fori_loop(0, STATES // (2 * PANEL), reorder, 0)

    def times(values, b, first, count):
        high, low = split(values)
        at = pl.ds(pl.multiple_of(b * COLS + first, 128), count)
        return mm3(high, low, rh[at], rl[at])

    got(fe, erecv, b_last, 1)
    got(fe, erecv, b_next, 0)
    got(fe, erecv, b_far, 0)
    got(fe, erecv, b_far, 1)
    turned = times(fe[0], 0, 0, EARLY) + times(fe[1], 1, 0, EARLY)
    turned = turned + (times(fe[2], 2, 0, EARLY) + times(fe[3], 3, 0, EARLY))
    turned_scaled = turned * m
    ghosts_out(2, turned_scaled)
    total = apply_own(turned_scaled)
    relay(fl, lrecv)
    ov[...] = times(late, band, EARLY, LATE)
    ov[top] += times(fl[b_last, top], b_last, EARLY, LATE)
    ov[bottom] += times(fl[b_next, bottom], b_next, EARLY, LATE)
    total = total + ghosts_in(2)
    sums_out(2, total)
    got(fl, lrecv, b_last, 1)
    ov[bottom] += times(fl[b_last, bottom], b_last, EARLY, LATE)
    got(fl, lrecv, b_next, 0)
    ov[top] += times(fl[b_next, top], b_next, EARLY, LATE)
    ov[...] += scale * (m * (total[FIRST:] + sums_in(2)) - root_b * turned)
    got(fl, lrecv, b_far, 0)
    ov[top] += times(fl[b_far, top], b_far, EARLY, LATE)
    got(fl, lrecv, b_far, 1)
    ov[bottom] += times(fl[b_far, bottom], b_far, EARLY, LATE)

    for copy in sends:
        copy.wait_send()


def shards(states, inv_mass, cell_ham, cell_nodes, send_up, send_down, owner, rotation_store):
    dma = pltpu.SemaphoreType.DMA
    vmem = pltpu.VMEM
    edges = [vmem((2 * GHOST, n), f32) for n in (COLS, LATE, COLS) for _ in range(4)]
    return pl.pallas_call(
        kernel,
        out_shape=vmem((OWN, COLS), f32),
        in_specs=[pl.BlockSpec(memory_space=pl.ANY)] * 8,
        out_specs=pl.BlockSpec(memory_space=pltpu.VMEM),
        scratch_shapes=[
            vmem((OWN, COLS), f32),
            vmem((1, OWN), f32),
            vmem((CELLS, CN, CN), f32),
            vmem((CELLS, CN), jnp.int32),
            vmem((1, GHOST), jnp.int32),
            vmem((1, GHOST), jnp.int32),
            pltpu.SMEM((64,), jnp.int32),
            vmem((64, PANEL, COLS), f32),
            *edges,
            vmem((EXT, EXT), f32),
            vmem((EXT, EXT), bf16),
            vmem((EXT, EXT), bf16),
            vmem((4, OWN, EARLY), f32),
            vmem((4, OWN, LATE), f32),
            vmem((STATES, COLS), bf16),
            vmem((STATES, COLS), bf16),
            dma((8,)),
            dma((32,)),
            dma((4, 2)),
            dma((4, 2)),
            dma((4, 2)),
            dma((3, 4)),
            dma((3, 4)),
            dma((12,)),
            dma((4, 2)),
            dma((4, 2)),
        ],
        compiler_params=pltpu.CompilerParams(
            collective_id=0, has_side_effects=True, vmem_limit_bytes=56 * 1024 * 1024
        ),
    )(
        states,
        inv_mass.reshape(1, OWN),
        cell_ham,
        cell_nodes,
        send_up.reshape(1, GHOST),
        send_down.reshape(1, GHOST),
        owner,
        rotation_store,
    )


def solution(mesh):
    in_specs = (
        P("dom", "band"),
        P("dom"),
        P("dom", None, None),
        P("dom", None),
        P("dom"),
        P("dom"),
        P(),
        P("dom", None),
    )
    return jax.shard_map(
        shards, mesh=mesh, in_specs=in_specs, out_specs=P("dom", "band"), check_vma=False
    )
```
